32 devices in a mesh: rep: 2 (over y), cell: 4 (over x, core), gene: 4 (over z).
Axes of the slice: x: 2, y: 2, z: 4, core: 2. Of those that a mesh axis runs over, the one named last changes fastest.
Arguments:
- counts: int32 [4096, 5120], P('cell', 'gene'), may hold values from 0 to 63
- usage_init: float32 [8192, 200], P(('rep', 'cell')), parts along dimension 0, may hold values from 0.05 to 1
- program_init: float32 [400, 5120], P('rep', 'gene'), parts along dimension 0, may hold values from 0.05 to 1
Outputs:
- usage: float32 [8192, 200], P(('rep', 'cell')), parts along dimension 0
- program: float32 [400, 5120], P('rep', 'gene'), parts along dimension 0
The draws below stay inside these ranges and needn't reach their ends.
There are 2 independent parts, one for each index of `rep`. The reference program is written for one: setup_inputs(seed, part) draws one part's arguments, and reference() takes and returns one part's arrays. A program takes and returns all parts, laid end to end along the dimension named above; an argument that names none is the same for every part. Nothing has to cross between parts.
All inputs are finite; a program needn't handle non-finite values.
Results may differ from the reference program's by a relative error of at most 0.0001.
Values sent between devices are 32-bit elements; how exact they have to be, the bound alone decides.
A program may use at most 64 MiB of HBM per device.

```python
import math
import jax
import jax.numpy as jnp
import numpy as np
from jax import lax

GENES = 5120
K = 200
ITERS = 2
CELLS = 4096


def set_ends(entries, stream_key, low, high):
    shape = entries.shape
    index_at = [jax.random.randint(jax.random.fold_in(stream_key, axis), (), 0, shape[axis]) for axis in range(len(shape))]
    entries = entries.at[tuple(index_at)].set(low)
    longest = shape.index(max(shape))
    index_at[longest] = (index_at[longest] + 1) % shape[longest]
    return entries.at[tuple(index_at)].set(high)


def level_of(key, dims, pieces, least, high):
    factor_of, own = 1.0, jax.random.fold_in(key, 6)
    for axis_at, parts in pieces:
        draws = jnp.exp(jax.random.uniform(jax.random.fold_in(own, axis_at), (parts,), jnp.float32, least / len(pieces), high / len(pieces)))
        factor_of = factor_of * jnp.repeat(draws, dims[axis_at] // parts).reshape([-1 if axis == axis_at else 1 for axis in range(len(dims))])
    return factor_of


def rank_bounds(number_of, lean):
    portions = [(1 << 20) // math.isqrt(grade ** lean) + 1 for grade in range(1, number_of + 1)]
    scale = 1 + sum(portions) // (1 << 30)
    return np.cumsum(np.array([max(1, weight // scale) for weight in portions]))


def skewed_ids(rng, dims, number_of, skew):
    grid = rank_bounds(number_of, skew)
    pick = jax.random.randint(jax.random.fold_in(rng, 1), dims, 0, int(grid[number_of - 1]))
    standing = jnp.searchsorted(jnp.asarray(grid, jnp.int32), pick, side="right")
    return jax.random.permutation(jax.random.fold_in(rng, 2), number_of)[standing].astype(jnp.int32)


def setup_inputs(seed: int = 0, part: int = 0) -> dict:
    keys = jax.random.split(jax.random.key(seed), 4)
    part_splits = jax.random.split(jax.random.fold_in(keys[3], part), 4)
    counts = set_ends(skewed_ids(keys[0], (CELLS, GENES), 64, 2), jax.random.fold_in(keys[0], 3), 0, 63).astype(jnp.int32)
    usage_init = jnp.clip(jnp.exp(math.log(1.0) - 2.9957323 * jax.random.uniform(part_splits[1], (CELLS, K), jnp.float32) ** level_of(part_splits[1], (CELLS, K), ((0, 4),), -0.2, 0.2)), 0.05, 1.0)
    program_init = jnp.clip(jnp.exp(math.log(1.0) - 2.9957323 * jax.random.uniform(part_splits[2], (K, GENES), jnp.float32) ** level_of(part_splits[2], (K, GENES), ((1, 4),), -0.2, 0.2)), 0.05, 1.0)
    return dict(counts=counts, usage_init=usage_init, program_init=program_init)


def reference(counts, usage_init, program_init):
    highest = lax.Precision.HIGHEST
    expression = counts.astype(jnp.float32)
    usage = usage_init
    program = program_init
    for iteration in range(ITERS):
        usage_top = jnp.dot(expression, program.T, precision=highest)
        program_gram = jnp.dot(program, program.T, precision=highest)
        usage = usage * usage_top / jnp.dot(usage, program_gram, precision=highest)
        program_top = jnp.dot(usage.T, expression, precision=highest)
        usage_gram = jnp.dot(usage.T, usage, precision=highest)
        program = program * program_top / jnp.dot(usage_gram, program, precision=highest)
    return usage, program
```

```python
import functools

import jax
import jax.numpy as jnp
from jax import lax
from jax.experimental import pallas as pl
from jax.experimental.pallas import tpu as pltpu
from jax.sharding import PartitionSpec as P

ITERS = 2
LANES = 128
WIDE = 2 * LANES
HOP = 4
GRAM_LAG, CORE_LAG, CHIP_LAG, SHARE_LAG = 3, 1, 4, 6

MESH = pl.DeviceIdType.MESH
f32 = jnp.float32


def dot(left, right, left_dim, right_dim):
    return lax.dot_general(
        left,
        right,
        (((left_dim,), (right_dim,)), ((), ())),
        preferred_element_type=f32,
    )


def parts(x):
    high = x.astype(jnp.bfloat16)
    return high, (x - high.astype(f32)).astype(jnp.bfloat16)


def dot_exact_right(left, right, right_dim):
    rows = left.shape[0]
    both = dot(jnp.concatenate(parts(left), 0), right, 1, right_dim)
    return both[:rows] + both[rows:]


def dot_three(left, right, right_dim):
    rows = left.shape[0]
    left_high, left_low = parts(left)
    right_high, right_low = parts(right)
    both = dot(jnp.concatenate([left_high, left_low], 0), right_high, 1, right_dim)
    return both[:rows] + (both[rows:] + dot(left_high, right_low, 1, right_dim))


def gram_blocks(n, rows):
    return [(r, 0) for r in range(n)] + [(r, 1) for r in range(n) if (r + 1) * rows > LANES]


def kernel(
    sizes,
    counts_ref, u_ref, p_ref, u_out, p_out,
    counts, e_ref,
    u_buf, p_buf, zp, z_in, z_out, z_mid, z_fin, g_own, g_all, gram,
    c_send, c_in, x_buf, x_fin, u_gram,
    zs_sem, zr_sem, gs_sem, gr_sem, cs_sem, cr_sem, xs_sem, xr_sem, fs_sem, fr_sem, in_sem,
):
    n_gene, n_cell, n, rows, cells, genes, real_genes, n_slots = sizes
    k = n * rows
    n_chip, reach = n_cell // 2, n_gene // 2
    subs = cells // WIDE
    half_genes = genes // 2
    blocks = gram_blocks(n, rows)
    lead = 2 * subs
    n_pieces = n * subs + n_slots

    z = lax.axis_index("gene")
    cell = lax.axis_index("cell")
    core = lax.rem(cell, 2)
    chip = cell // 2
    other = 1 - core
    low = z < reach
    far = jnp.where(low, reach - 1 - z, z - reach)
    inner = jnp.where(low, z + 1, z - 1)
    outer = jnp.where(low, z - 1, z + 1)
    middle, edge = far == 0, far == reach - 1

    def load(s):
        at_row = pl.ds(pl.multiple_of(s * WIDE, WIDE), WIDE)
        return pltpu.make_async_copy(counts_ref.at[at_row], counts.at[s], in_sem.at[s])

    for s in range(subs):
        load(s).start()

    barrier = pltpu.get_barrier_semaphore()
    pl.semaphore_signal(barrier, inc=1, device_id={"gene": inner}, device_id_type=MESH)

    @pl.when(jnp.logical_not(edge))
    def _():
        pl.semaphore_signal(barrier, inc=1, device_id={"gene": outer}, device_id_type=MESH)

    for away in range(1, n_cell):
        peer = lax.rem(cell + away, n_cell)
        pl.semaphore_signal(barrier, inc=1, device_id={"cell": peer}, device_id_type=MESH)
    pl.semaphore_wait(barrier, n_cell + 1 - jnp.where(edge, 1, 0))

    u_buf[0] = u_ref[...]
    p_buf[0] = p_ref[...]

    def take_counts(s):
        load(s).wait()
        at_row = pl.ds(pl.multiple_of(s * WIDE, WIDE), WIDE)
        e_ref[at_row, :real_genes] = counts[s].astype(f32).astype(jnp.bfloat16)
        if real_genes < genes:
            e_ref[at_row, real_genes:] = jnp.zeros((WIDE, genes - real_genes), jnp.bfloat16)

    def remote(src, dst, send, recv, to):
        return pltpu.make_async_remote_copy(
            src_ref=src, dst_ref=dst, send_sem=send, recv_sem=recv, device_id=to, device_id_type=MESH
        )

    def inward(it, c):
        return remote(z_out.at[it, c], z_in.at[it, c], zs_sem.at[it, 0, c], zr_sem.at[it, 0, c], {"gene": inner})

    def across(it, c):
        return remote(z_out.at[it, c], z_mid.at[it, c], zs_sem.at[it, 0, c], zr_sem.at[it, 1, c], {"gene": inner})

    def outward(it, c):
        return remote(z_fin.at[it, c], z_fin.at[it, c], zs_sem.at[it, 1, c], zr_sem.at[it, 1, c], {"gene": outer})

    def spread(it, s, away):
        to = lax.rem(cell + away, n_cell)
        mine = g_all.at[it, s * n_cell + cell]
        return remote(mine, mine, gs_sem.at[it, s, away - 1], gr_sem.at[it, s, away - 1], {"cell": to})

    def spread_from(it, s, away):
        to = lax.rem(cell + n_cell - away, n_cell)
        theirs = g_all.at[it, s * n_cell + to]
        return remote(theirs, theirs, gs_sem.at[it, s, away - 1], gr_sem.at[it, s, away - 1], {"cell": to})

    def to_core(it, j):
        return remote(
            c_send.at[it, j, other], c_in.at[it, j], cs_sem.at[it, j], cr_sem.at[it, j], {"cell": chip * 2 + other}
        )

    def to_chip(it, j, away):
        to = lax.rem(chip + away, n_chip)
        mine = x_buf.at[it, j, chip]
        return remote(mine, mine, xs_sem.at[it, j, away - 1], xr_sem.at[it, j, away - 1], {"cell": to * 2 + core})

    def from_chip(it, j, away):
        to = lax.rem(chip + n_chip - away, n_chip)
        theirs = x_buf.at[it, j, to]
        return remote(theirs, theirs, xs_sem.at[it, j, away - 1], xr_sem.at[it, j, away - 1], {"cell": to * 2 + core})

    def share(it, j, which):
        piece = x_fin.at[it, j, which]
        return remote(piece, piece, fs_sem.at[it, j], fr_sem.at[it, j], {"cell": chip * 2 + other})

    def gather_in(it, c):
        @pl.when(edge)
        def _():
            z_out[it, c] = zp[c]

        @pl.when(jnp.logical_not(edge))
        def _():
            inward(it, c).wait_recv()
            z_out[it, c] = zp[c] + z_in[it, c]

        @pl.when(middle)
        def _():
            across(it, c).start()

        @pl.when(jnp.logical_not(middle))
        def _():
            inward(it, c).start()

    def spread_out(it, c):
        @pl.when(middle)
        def _():
            across(it, c).wait_recv()
            z_fin[it, c] = z_out[it, c] + z_mid[it, c]

        @pl.when(jnp.logical_not(middle))
        def _():
            outward(it, c).wait_recv()

        @pl.when(jnp.logical_not(edge))
        def _():
            outward(it, c).start()

    def numerator(it, q):
        j, s = q // subs, lax.rem(q, subs)
        at_row = pl.ds(pl.multiple_of(s * WIDE, WIDE), WIDE)
        zp[q + jnp.where(q >= lead, n_slots, 0)] = dot_exact_right(p_buf[it, j], e_ref[at_row, :], 1)

    def own_gram(it):
        whole = p_buf[it].reshape(k, genes)
        own = dot_three(whole, whole, 1)
        own = jnp.concatenate([own, jnp.zeros((k, 2 * LANES - k), f32)], 1)
        for i in range(2 * n_slots * n_cell):
            r, h = blocks[min(i, len(blocks) - 1)]
            at = (i % 2) * LANES
            g_own[i // 2, :, at:at + LANES] = own[r * rows:(r + 1) * rows, h * LANES:(h + 1) * LANES]
        for s in range(n_slots):
            zp[lead + s] = g_own[s * n_cell + cell]

    def spread_gram(it):
        for s in range(n_slots):
            g_all[it, s * n_cell + cell] = z_fin[it, lead + s]
            for away in range(1, n_cell):
                spread(it, s, away).start()

    def join_gram(it):
        for s in range(n_slots):
            for away in range(1, n_cell):
                spread_from(it, s, away).wait_recv()
        none = jnp.zeros((rows, LANES), f32)
        lines = []
        for r in range(n):
            halves = []
            for h in range(2):
                if (r, h) in blocks:
                    i = blocks.index((r, h))
                    halves.append(g_all[it, i // 2, :, (i % 2) * LANES:(i % 2 + 1) * LANES])
                else:
                    halves.append(none)
            lines.append(jnp.concatenate(halves, 1))
        lines.append(jnp.zeros((2 * LANES - k, 2 * LANES), f32))
        known = jnp.concatenate(lines, 0)
        first = min(r for r, h in blocks if h == 1) * rows
        row = lax.broadcasted_iota(jnp.int32, known.shape, 0)
        column = lax.broadcasted_iota(jnp.int32, known.shape, 1)
        missing = jnp.logical_and(row < first, column >= LANES)
        full = jnp.where(missing, known.T, known)
        for r in range(n):
            gram[r] = full[r * rows:(r + 1) * rows]

    def update_usage(it, j):
        first = j * subs + jnp.where(j >= 2, n_slots, 0)
        top = jnp.concatenate([z_fin[it, first + s] for s in range(subs)], 1)
        old = u_buf[it].reshape(k, cells)
        new = u_buf[it, j] * top / dot_three(gram[j][:, :k], old, 0)
        u_buf[it + 1, j] = new

        def half(h):
            at = pl.ds(pl.multiple_of(h * half_genes, LANES), half_genes)
            c_send[it, j, h, :, :half_genes] = dot_exact_right(new, e_ref[:, at], 0)

        own = dot_three(new, u_buf[it + 1].reshape(k, cells), 1)
        c_send[it, j, 0, :, half_genes:] = own[:, :LANES]
        c_send[it, j, 1, :, half_genes:] = jnp.concatenate(
            [own[:, LANES:], jnp.zeros((rows, 2 * LANES - k), f32)], 1
        )
        half(other)
        to_core(it, j).start()
        half(core)

    def update_program(it, j):
        top = jnp.concatenate([x_fin[it, j, h, :, :half_genes] for h in range(2)], 1)
        old = p_buf[it].reshape(k, genes)
        at_row = pl.ds(pl.multiple_of(j * rows, rows), rows)
        new = p_buf[it, j] * top / dot_three(u_gram[at_row, :][:, :k], old, 0)
        if real_genes < genes:
            inside = lax.broadcasted_iota(jnp.int32, (rows, genes), 1) < real_genes
            new = jnp.where(inside, new, 0.0)
        return new

    def settle_pieces(it):
        def pieces(c, carry):
            inward(it, c).wait_send()

            @pl.when(jnp.logical_not(edge))
            def _():
                outward(it, c).wait_send()

            return carry

        lax.fori_loop(0, n_pieces, pieces, 0)
        for s in range(n_slots):
            for away in range(1, n_cell):
                spread(it, s, away).wait_send()

    turns = [
        max((j + 1) * subs + (n_slots if j >= 2 else 0) - 1, lead + n_slots + GRAM_LAG + 2 * j) for j in range(n)
    ]
    program_turns = [j * lead // n for j in range(n)]

    def step(it, carry):
        u_buf[it + 1] = jnp.zeros(u_buf.shape[1:], f32)
        inward_lag = (reach - 1 - far) * HOP
        done = (reach + far) * HOP
        ticks = (2 * reach - 1) * HOP + turns[-1] + SHARE_LAG + 1

        def tick(t, carry):
            def at(lag, count, act):
                @pl.when(jnp.logical_and(t >= lag, t < lag + count))
                def _():
                    act(t - lag)

            def at_turn(since, when, act):
                hit, j = since == when[0], 0
                for i in range(1, n):
                    now = since == when[i]
                    hit, j = jnp.logical_or(hit, now), jnp.where(now, i, j)

                @pl.when(hit)
                def _():
                    act(j)

            def next_program(j):
                p_buf[it, j] = update_program(it - 1, j)

            @pl.when(jnp.logical_and(it == 0, t < subs))
            def _():
                take_counts(t)

            at_turn(jnp.where(it > 0, t, -1), program_turns, next_program)
            q = t - jnp.where(t >= lead + n_slots, n_slots, 0)
            a_piece = jnp.logical_and(jnp.logical_or(t < lead, t >= lead + n_slots), q < n * subs)

            @pl.when(a_piece)
            def _():
                numerator(it, q)

            @pl.when(t == lead)
            def _():
                own_gram(it)

            at(inward_lag, n_pieces, lambda c: gather_in(it, c))
            at(done, n_pieces, lambda c: spread_out(it, c))

            @pl.when(t == done + lead + n_slots - 1)
            def _():
                spread_gram(it)

            @pl.when(t == done + lead + n_slots + GRAM_LAG)
            def _():
                join_gram(it)

            at_turn(t - done, turns, lambda j: update_usage(it, j))

            def join_core(j):
                to_core(it, j).wait_recv()
                x_buf[it, j, chip] = c_send[it, j, core] + c_in[it, j]
                for away in range(1, n_chip):
                    to_chip(it, j, away).start()

            at_turn(t - done - CORE_LAG, turns, join_core)

            @pl.when(t == done + CORE_LAG + turns[-1])
            def _():
                settle_pieces(it)
            def join_chip(j):
                for away in range(1, n_chip):
                    from_chip(it, j, away).wait_recv()
                total = x_buf[it, j, 0]
                for peer in range(1, n_chip):
                    total = total + x_buf[it, j, peer]
                x_fin[it, j, core] = total
                share(it, j, core).start()

            at_turn(t - done - CHIP_LAG, turns, join_chip)
            at_turn(t - done - SHARE_LAG, turns, lambda j: share(it, j, other).wait_recv())
            return carry

        lax.fori_loop(0, ticks, tick, 0)

        columns = lax.broadcasted_iota(jnp.int32, (rows, 2 * LANES), 1)
        lower, strict = [], []
        for r in range(n):
            block = jnp.concatenate([x_fin[it, r, h, :, half_genes:] for h in range(2)], 1)
            lower.append(jnp.where(columns < (r + 1) * rows, block, 0.0))
            strict.append(jnp.where(columns < r * rows, block, 0.0))
        pad = jnp.zeros((2 * LANES - k, 2 * LANES), f32)
        u_gram[...] = jnp.concatenate(lower + [pad], 0) + jnp.concatenate(strict + [pad], 0).T
        return carry

    lax.fori_loop(0, ITERS, step, 0)

    def last_program(j, carry):
        p_out[j] = update_program(ITERS - 1, j)
        return carry

    lax.fori_loop(0, n, last_program, 0)
    u_out[...] = u_buf[ITERS]

    def settle(it, carry):
        def chunks(j, carry):
            to_core(it, j).wait_send()
            for away in range(1, n_chip):
                to_chip(it, j, away).wait_send()
            share(it, j, core).wait_send()
            return carry

        lax.fori_loop(0, n, chunks, 0)
        return carry

    lax.fori_loop(0, ITERS, settle, 0)


def body(mesh, counts, usage_init, program_init):
    cells, k = usage_init.shape
    real_genes = program_init.shape[1]
    n_gene, n_cell = mesh.shape["gene"], mesh.shape["cell"]
    n_chip = n_cell // 2
    rows = max(r for r in range(8, 41, 8) if k % r == 0)
    n = k // rows
    genes = -(-real_genes // (2 * LANES)) * 2 * LANES
    n_slots = -(-len(gram_blocks(n, rows)) // (2 * n_cell))
    n_pieces = n * (cells // WIDE) + n_slots
    width = genes // 2 + LANES

    program = program_init
    if genes > real_genes:
        program = jnp.pad(program, ((0, 0), (0, genes - real_genes)))

    sizes = (n_gene, n_cell, n, rows, cells, genes, real_genes, n_slots)
    vmem = pl.BlockSpec(memory_space=pltpu.VMEM)
    dma = pltpu.SemaphoreType.DMA
    usage, program = pl.pallas_call(
        functools.partial(kernel, sizes),
        out_shape=[
            jax.ShapeDtypeStruct((n, rows, cells), f32),
            jax.ShapeDtypeStruct((n, rows, genes), f32),
        ],
        in_specs=[pl.BlockSpec(memory_space=pl.ANY), vmem, vmem],
        out_specs=[vmem] * 2,
        scratch_shapes=[
            pltpu.VMEM((cells // WIDE, WIDE, real_genes), jnp.int32),
            pltpu.VMEM((cells, genes), jnp.bfloat16),
            pltpu.VMEM((ITERS + 1, n, rows, cells), f32),
            pltpu.VMEM((ITERS + 1, n, rows, genes), f32),
            pltpu.VMEM((n_pieces, rows, WIDE), f32),
            pltpu.VMEM((ITERS, n_pieces, rows, WIDE), f32),
            pltpu.VMEM((ITERS, n_pieces, rows, WIDE), f32),
            pltpu.VMEM((ITERS, n_pieces, rows, WIDE), f32),
            pltpu.VMEM((ITERS, n_pieces, rows, WIDE), f32),
            pltpu.VMEM((n_slots * n_cell, rows, WIDE), f32),
            pltpu.VMEM((ITERS, n_slots * n_cell, rows, WIDE), f32),
            pltpu.VMEM((n, rows, 2 * LANES), f32),
            pltpu.VMEM((ITERS, n, 2, rows, width), f32),
            pltpu.VMEM((ITERS, n, rows, width), f32),
            pltpu.VMEM((ITERS, n, n_chip, rows, width), f32),
            pltpu.VMEM((ITERS, n, 2, rows, width), f32),
            pltpu.VMEM((2 * LANES, 2 * LANES), f32),
            dma((ITERS, 2, n_pieces)),
            dma((ITERS, 2, n_pieces)),
            dma((ITERS, n_slots, n_cell - 1)),
            dma((ITERS, n_slots, n_cell - 1)),
            dma((ITERS, n)),
            dma((ITERS, n)),
            dma((ITERS, n, max(n_chip - 1, 1))),
            dma((ITERS, n, max(n_chip - 1, 1))),
            dma((ITERS, n)),
            dma((ITERS, n)),
            dma((cells // WIDE,)),
        ],
        compiler_params=pltpu.CompilerParams(
            collective_id=0, has_side_effects=True, vmem_limit_bytes=60 * 1024 * 1024
        ),
    )(
        counts,
        usage_init.T.reshape(n, rows, cells),
        program.reshape(n, rows, genes),
    )
    usage = usage.reshape(k, cells).T
    program = program.reshape(k, genes)[:, :real_genes]
    return usage, program


def solution(mesh):
    return jax.shard_map(
        functools.partial(body, mesh),
        mesh=mesh,
        in_specs=(P("cell", "gene"), P(("rep", "cell"), None), P("rep", "gene")),
        out_specs=(P(("rep", "cell"), None), P("rep", "gene")),
        check_vma=False,
    )
```

```python
import functools

import jax
import jax.numpy as jnp
from jax import lax
from jax.experimental import pallas as pl
from jax.experimental.pallas import tpu as pltpu
from jax.sharding import PartitionSpec as P

ITERS = 2
LANES = 128
WIDE = 2 * LANES
HOP, PACE = 8, 2
GRAM_LAG, CORE_LAG, CHIP_LAG, SHARE_LAG = 7, 3, 13, 16
JOIN_LAG, SETTLE_LAG = 8, 6

MESH = pl.DeviceIdType.MESH
f32 = jnp.float32


def dot(left, right, left_dim, right_dim):
    return lax.dot_general(
        left,
        right,
        (((left_dim,), (right_dim,)), ((), ())),
        preferred_element_type=f32,
    )


def parts(x):
    high = x.astype(jnp.bfloat16)
    return high, (x - high.astype(f32)).astype(jnp.bfloat16)


def dot_exact_right(left, right, right_dim):
    rows = left.shape[0]
    both = dot(jnp.concatenate(parts(left), 0), right, 1, right_dim)
    return both[:rows] + both[rows:]


def dot_three(left, right, right_dim):
    rows = left.shape[0]
    left_high, left_low = parts(left)
    right_high, right_low = parts(right)
    both = dot(jnp.concatenate([left_high, left_low], 0), right_high, 1, right_dim)
    return both[:rows] + (both[rows:] + dot(left_high, right_low, 1, right_dim))


def gram_blocks(n, rows):
    return [(r, 0) for r in range(n)] + [(r, 1) for r in range(n) if (r + 1) * rows > LANES]


def kernel(
    sizes,
    counts_ref, u_ref, p_ref, u_out, p_out,
    counts, e_ref,
    u_buf, p_buf, zp, z_in, z_out, z_mid, z_fin, g_own, g_all, gram, below,
    c_send, c_in, x_buf, x_fin, last_gram, u_gram,
    zs_sem, zr_sem, gs_sem, gr_sem, cs_sem, cr_sem, xs_sem, xr_sem, fs_sem, fr_sem, ds_sem, dr_sem,
    in_sem, start_sem, u_sem, p_sem,
):
    n_gene, n_cell, n, rows, cells, genes, real_genes, n_slots = sizes
    k = n * rows
    n_chip, reach = n_cell // 2, n_gene // 2
    subs = cells // WIDE
    half_genes = genes // 2
    blocks = gram_blocks(n, rows)
    lead_chunk = -(-(n - 1) // subs)
    lead = lead_chunk * subs
    n_pieces = n * subs + n_slots
    final = n - 1

    z = lax.axis_index("gene")
    cell = lax.axis_index("cell")
    core = lax.rem(cell, 2)
    chip = cell // 2
    other = 1 - core
    low = z < reach
    far = jnp.where(low, reach - 1 - z, z - reach)
    inner = jnp.where(low, z + 1, z - 1)
    outer = jnp.where(low, z - 1, z + 1)
    middle, edge = far == 0, far == reach - 1

    def load(s):
        at_row = pl.ds(pl.multiple_of(s * WIDE, WIDE), WIDE)
        return pltpu.make_async_copy(counts_ref.at[at_row], counts.at[s], in_sem.at[s])

    load_program = pltpu.make_async_copy(p_ref, p_buf.at[0], start_sem.at[0])
    load_usage = pltpu.make_async_copy(u_ref, u_buf.at[0], start_sem.at[1])
    load_program.start()
    for s in range(subs):
        load(s).start()
    load_usage.start()

    barrier = pltpu.get_barrier_semaphore()
    pl.semaphore_signal(barrier, inc=1, device_id={"gene": inner}, device_id_type=MESH)

    @pl.when(jnp.logical_not(edge))
    def _():
        pl.semaphore_signal(barrier, inc=1, device_id={"gene": outer}, device_id_type=MESH)

    for away in range(1, n_cell):
        peer = lax.rem(cell + away, n_cell)
        pl.semaphore_signal(barrier, inc=1, device_id={"cell": peer}, device_id_type=MESH)

    def take_counts(s):
        load(s).wait()
        at_row = pl.ds(pl.multiple_of(s * WIDE, WIDE), WIDE)
        e_ref[at_row, :real_genes] = counts[s].astype(f32).astype(jnp.bfloat16)
        if real_genes < genes:
            e_ref[at_row, real_genes:] = jnp.zeros((WIDE, genes - real_genes), jnp.bfloat16)

    def clear(i, carry):
        u_buf[1 + i // n, lax.rem(i, n)] = jnp.zeros((rows, cells), f32)
        return carry

    lax.fori_loop(0, ITERS * n, clear, 0)
    load_program.wait()
    early = min(2, subs)
    lax.fori_loop(0, early, lambda s, carry: (take_counts(s), carry)[1], 0)
    pl.semaphore_wait(barrier, n_cell + 1 - jnp.where(edge, 1, 0))

    def remote(src, dst, send, recv, to):
        return pltpu.make_async_remote_copy(
            src_ref=src, dst_ref=dst, send_sem=send, recv_sem=recv, device_id=to, device_id_type=MESH
        )

    def inward(it, c):
        return remote(z_out.at[it, c], z_in.at[it, c], zs_sem.at[it, 0, c], zr_sem.at[it, 0, c], {"gene": inner})

    def across(it, c):
        return remote(z_out.at[it, c], z_mid.at[it, c], zs_sem.at[it, 0, c], zr_sem.at[it, 1, c], {"gene": inner})

    def outward(it, c):
        return remote(z_fin.at[it, c], z_fin.at[it, c], zs_sem.at[it, 1, c], zr_sem.at[it, 1, c], {"gene": outer})

    def spread(it, s, away):
        to = lax.rem(cell + away, n_cell)
        mine = g_all.at[it, s * n_cell + cell]
        return remote(mine, mine, gs_sem.at[it, s, away - 1], gr_sem.at[it, s, away - 1], {"cell": to})

    def spread_from(it, s, away):
        to = lax.rem(cell + n_cell - away, n_cell)
        theirs = g_all.at[it, s * n_cell + to]
        return remote(theirs, theirs, gs_sem.at[it, s, away - 1], gr_sem.at[it, s, away - 1], {"cell": to})

    def direct(it, away):
        to = lax.rem(cell + away, n_cell)
        mine = last_gram.at[it, cell]
        return remote(mine, mine, ds_sem.at[it, away - 1], dr_sem.at[it, away - 1], {"cell": to})

    def direct_from(it, away):
        to = lax.rem(cell + n_cell - away, n_cell)
        theirs = last_gram.at[it, to]
        return remote(theirs, theirs, ds_sem.at[it, away - 1], dr_sem.at[it, away - 1], {"cell": to})

    def columns(last):
        return pl.ds(0, half_genes if last else half_genes + LANES)

    def to_core(it, j, last):
        at = columns(last)
        return remote(
            c_send.at[it, j, other, :, at], c_in.at[it, j, :, at], cs_sem.at[it, j], cr_sem.at[it, j],
            {"cell": chip * 2 + other},
        )

    def to_chip(it, j, away, last):
        to = lax.rem(chip + away, n_chip)
        mine = x_buf.at[it, j, chip, :, columns(last)]
        return remote(mine, mine, xs_sem.at[it, j, away - 1], xr_sem.at[it, j, away - 1], {"cell": to * 2 + core})

    def from_chip(it, j, away, last):
        to = lax.rem(chip + n_chip - away, n_chip)
        theirs = x_buf.at[it, j, to, :, columns(last)]
        return remote(theirs, theirs, xs_sem.at[it, j, away - 1], xr_sem.at[it, j, away - 1], {"cell": to * 2 + core})

    def share(it, j, which, last):
        piece = x_fin.at[it, j, which, :, columns(last)]
        return remote(piece, piece, fs_sem.at[it, j], fr_sem.at[it, j], {"cell": chip * 2 + other})

    def put_usage(j):
        return pltpu.make_async_copy(u_buf.at[ITERS, j], u_out.at[j], u_sem.at[j])

    def put_program(j):
        return pltpu.make_async_copy(p_buf.at[ITERS, j], p_out.at[j], p_sem.at[j])

    def gather_in(it, c):
        @pl.when(edge)
        def _():
            z_out[it, c] = zp[c]

        @pl.when(jnp.logical_not(edge))
        def _():
            inward(it, c).wait_recv()
            z_out[it, c] = zp[c] + z_in[it, c]

        @pl.when(middle)
        def _():
            across(it, c).start()

        @pl.when(jnp.logical_not(middle))
        def _():
            inward(it, c).start()

    def spread_out(it, c):
        @pl.when(middle)
        def _():
            across(it, c).wait_recv()
            z_fin[it, c] = z_out[it, c] + z_mid[it, c]

        @pl.when(jnp.logical_not(middle))
        def _():
            outward(it, c).wait_recv()

        @pl.when(jnp.logical_not(edge))
        def _():
            outward(it, c).start()

    def numerator(it, q):
        j, s = q // subs, lax.rem(q, subs)
        at_row = pl.ds(pl.multiple_of(s * WIDE, WIDE), WIDE)
        zp[q + jnp.where(q >= lead, n_slots, 0)] = dot_exact_right(p_buf[it, j], e_ref[at_row, :], 1)

    def own_gram(it):
        whole = p_buf[it].reshape(k, genes)
        own = dot_three(whole, whole, 1)
        own = jnp.concatenate([own, jnp.zeros((k, 2 * LANES - k), f32)], 1)
        for i in range(2 * n_slots * n_cell):
            r, h = blocks[min(i, len(blocks) - 1)]
            at = (i % 2) * LANES
            g_own[i // 2, :, at:at + LANES] = own[r * rows:(r + 1) * rows, h * LANES:(h + 1) * LANES]
        for s in range(n_slots):
            zp[lead + s] = g_own[s * n_cell + cell]

    def spread_gram(it):
        for s in range(n_slots):
            g_all[it, s * n_cell + cell] = z_fin[it, lead + s]
            for away in range(1, n_cell):
                spread(it, s, away).start()

    def join_gram(it):
        for s in range(n_slots):
            for away in range(1, n_cell):
                spread_from(it, s, away).wait_recv()
        none = jnp.zeros((rows, LANES), f32)
        lines = []
        for r in range(n):
            halves = []
            for h in range(2):
                if (r, h) in blocks:
                    i = blocks.index((r, h))
                    halves.append(g_all[it, i // 2, :, (i % 2) * LANES:(i % 2 + 1) * LANES])
                else:
                    halves.append(none)
            lines.append(jnp.concatenate(halves, 1))
        lines.append(jnp.zeros((2 * LANES - k, 2 * LANES), f32))
        known = jnp.concatenate(lines, 0)
        first = min(r for r, h in blocks if h == 1) * rows
        row = lax.broadcasted_iota(jnp.int32, known.shape, 0)
        column = lax.broadcasted_iota(jnp.int32, known.shape, 1)
        missing = jnp.logical_and(row < first, column >= LANES)
        full = jnp.where(missing, known.T, known)
        for r in range(n):
            gram[r] = full[r * rows:(r + 1) * rows]

    def usage_below(it, j):
        below[j] = dot_three(gram[j][:, :k], u_buf[it].reshape(k, cells), 0)

    def update_usage(it, j, last):
        first = j * subs + jnp.where(j >= lead_chunk, n_slots, 0)
        top = jnp.concatenate([z_fin[it, first + s] for s in range(subs)], 1)
        new = u_buf[it, j] * top / below[j]
        u_buf[it + 1, j] = new

        @pl.when(it == ITERS - 1)
        def _():
            put_usage(j).start()

        def half(h):
            at = pl.ds(pl.multiple_of(h * half_genes, LANES), half_genes)
            c_send[it, j, h, :, :half_genes] = dot_exact_right(new, e_ref[:, at], 0)

        own = dot_three(new, u_buf[it + 1].reshape(k, cells), 1)
        pad = jnp.zeros((rows, 2 * LANES - k), f32)
        if last:
            last_gram[it, cell] = jnp.concatenate([own, pad], 1)
            for away in range(1, n_cell):
                direct(it, away).start()
        else:
            c_send[it, j, 0, :, half_genes:] = own[:, :LANES]
            c_send[it, j, 1, :, half_genes:] = jnp.concatenate([own[:, LANES:], pad], 1)
        half(other)
        to_core(it, j, last).start()
        half(core)

    def join_core(it, j, last):
        at = columns(last)
        to_core(it, j, last).wait_recv()
        x_buf[it, j, chip, :, at] = c_send[it, j, core, :, at] + c_in[it, j, :, at]
        for away in range(1, n_chip):
            to_chip(it, j, away, last).start()

    def join_chip(it, j, last):
        at = columns(last)
        for away in range(1, n_chip):
            from_chip(it, j, away, last).wait_recv()
        total = x_buf[it, j, 0, :, at]
        for peer in range(1, n_chip):
            total = total + x_buf[it, j, peer, :, at]
        x_fin[it, j, core, :, at] = total
        share(it, j, core, last).start()

    def join_share(it, j, last):
        share(it, j, other, last).wait_recv()

    def join_usage_gram(it):
        for away in range(1, n_cell):
            direct_from(it, away).wait_recv()
        ending = last_gram[it, 0]
        for peer in range(1, n_cell):
            ending = ending + last_gram[it, peer]
        at_column = lax.broadcasted_iota(jnp.int32, (rows, 2 * LANES), 1)
        lower, strict = [], []
        for r in range(n):
            if r == final:
                block = ending
            else:
                block = jnp.concatenate([x_fin[it, r, h, :, half_genes:] for h in range(2)], 1)
            lower.append(jnp.where(at_column < (r + 1) * rows, block, 0.0))
            strict.append(jnp.where(at_column < r * rows, block, 0.0))
        pad = jnp.zeros((2 * LANES - k, 2 * LANES), f32)
        u_gram[...] = jnp.concatenate(lower + [pad], 0) + jnp.concatenate(strict + [pad], 0).T

    def update_program(it, j):
        top = jnp.concatenate([x_fin[it, j, h, :, :half_genes] for h in range(2)], 1)
        old = p_buf[it].reshape(k, genes)
        at_row = pl.ds(pl.multiple_of(j * rows, rows), rows)
        new = p_buf[it, j] * top / dot_three(u_gram[at_row, :][:, :k], old, 0)
        if real_genes < genes:
            inside = lax.broadcasted_iota(jnp.int32, (rows, genes), 1) < real_genes
            new = jnp.where(inside, new, 0.0)
        p_buf[it + 1, j] = new

        @pl.when(it == ITERS - 1)
        def _():
            put_program(j).start()

    def settle_pieces(it):
        def pieces(c, carry):
            inward(it, c).wait_send()

            @pl.when(jnp.logical_not(edge))
            def _():
                outward(it, c).wait_send()

            return carry

        lax.fori_loop(0, n_pieces, pieces, 0)
        for s in range(n_slots):
            for away in range(1, n_cell):
                spread(it, s, away).wait_send()

    def settle_chunks(it):
        def chunks(j, last):
            to_core(it, j, last).wait_send()
            for away in range(1, n_chip):
                to_chip(it, j, away, last).wait_send()
            share(it, j, core, last).wait_send()

        lax.fori_loop(0, final, lambda j, carry: (chunks(j, False), carry)[1], 0)
        chunks(final, True)
        for away in range(1, n_cell):
            direct(it, away).wait_send()

    place = [(j + 1) * subs - 1 + (n_slots if j >= lead_chunk else 0) for j in range(n)]
    gram_place = PACE * (lead + n_slots - 1)
    joined = gram_place + GRAM_LAG
    turns = [max(PACE * place[j], joined + 1 + 2 * j) for j in range(n)]
    below_turns = [joined + 2 * j for j in range(n)]
    inward_lag = (reach - 1 - far) * HOP
    done = (reach + far) * HOP
    period = (2 * reach - 1) * HOP + turns[final] + JOIN_LAG
    ticks = ITERS * period + n
    pace_in = jnp.where(edge, 1, PACE)

    def tick(t, carry):
        def frame(start):
            it = 0
            for i in range(1, ITERS):
                it = it + jnp.where(t >= start + i * period, 1, 0)
            return it, t - start - it * period

        def at_turn(start, when, act):
            it, since = frame(start)
            hit, j = since == when[0], 0
            for i in range(1, len(when)):
                now = since == when[i]
                hit, j = jnp.logical_or(hit, now), jnp.where(now, i, j)

            @pl.when(hit)
            def _():
                act(it, j)

        def at_chunk(start, when, lag, last_lag, act):
            at_turn(start + lag, when[:final], lambda it, j: act(it, j, False))
            at_turn(start + last_lag, when[final:], lambda it, j: act(it, final, True))

        def at_time(start, act):
            at_turn(start, [0], lambda it, j: act(it))

        @pl.when(jnp.logical_and(t >= early, t < subs))
        def _():
            take_counts(t)

        at_chunk(done, turns, CORE_LAG, CORE_LAG, join_core)
        at_chunk(done, turns, CHIP_LAG, JOIN_LAG + 2, join_chip)
        at_chunk(done, turns, SHARE_LAG, JOIN_LAG + final, join_share)
        at_time(period, join_usage_gram)
        at_turn(period, list(range(n)), update_program)

        it, since = frame(0)
        q = since - jnp.where(since >= lead + n_slots, n_slots, 0)

        @pl.when(jnp.logical_and(jnp.logical_or(since < lead, since >= lead + n_slots), q < n * subs))
        def _():
            numerator(it, q)

        @pl.when(since == lead)
        def _():
            own_gram(it)

        def at_pieces(start, pace, act):
            it, since = frame(start)
            c = since // pace

            @pl.when(jnp.logical_and(jnp.logical_and(since >= 0, c * pace == since), c < n_pieces))
            def _():
                act(it, c)

        it_in, since_in = frame(inward_lag)
        c_in_turn = jnp.where(edge, since_in, since_in // PACE)

        @pl.when(
            jnp.logical_and(
                jnp.logical_and(since_in >= 0, c_in_turn * pace_in == since_in), c_in_turn < n_pieces
            )
        )
        def _():
            gather_in(it_in, c_in_turn)

        at_pieces(done, PACE, spread_out)
        at_time(done + gram_place, spread_gram)
        at_time(done + joined, join_gram)
        at_turn(done, below_turns, usage_below)
        at_chunk(done, turns, 0, 0, update_usage)
        at_time(done + turns[final] + SETTLE_LAG, settle_pieces)
        return carry

    load_usage.wait()
    lax.fori_loop(0, ticks, tick, 0)

    for it in range(ITERS):
        settle_chunks(it)
    for j in range(n):
        put_usage(j).wait()
        put_program(j).wait()


def body(mesh, counts, usage_init, program_init):
    cells, k = usage_init.shape
    real_genes = program_init.shape[1]
    n_gene, n_cell = mesh.shape["gene"], mesh.shape["cell"]
    n_chip = n_cell // 2
    rows = max(r for r in range(8, 41, 8) if k % r == 0)
    n = k // rows
    genes = -(-real_genes // (2 * LANES)) * 2 * LANES
    n_slots = -(-len(gram_blocks(n, rows)) // (2 * n_cell))
    n_pieces = n * (cells // WIDE) + n_slots
    width = genes // 2 + LANES

    program = program_init
    if genes > real_genes:
        program = jnp.pad(program, ((0, 0), (0, genes - real_genes)))

    sizes = (n_gene, n_cell, n, rows, cells, genes, real_genes, n_slots)
    anywhere = pl.BlockSpec(memory_space=pl.ANY)
    dma = pltpu.SemaphoreType.DMA
    usage, program = pl.pallas_call(
        functools.partial(kernel, sizes),
        out_shape=[
            jax.ShapeDtypeStruct((n, rows, cells), f32),
            jax.ShapeDtypeStruct((n, rows, genes), f32),
        ],
        in_specs=[anywhere] * 3,
        out_specs=[anywhere] * 2,
        scratch_shapes=[
            pltpu.VMEM((cells // WIDE, WIDE, real_genes), jnp.int32),
            pltpu.VMEM((cells, genes), jnp.bfloat16),
            pltpu.VMEM((ITERS + 1, n, rows, cells), f32),
            pltpu.VMEM((ITERS + 1, n, rows, genes), f32),
            pltpu.VMEM((n_pieces, rows, WIDE), f32),
            pltpu.VMEM((ITERS, n_pieces, rows, WIDE), f32),
            pltpu.VMEM((ITERS, n_pieces, rows, WIDE), f32),
            pltpu.VMEM((ITERS, n_pieces, rows, WIDE), f32),
            pltpu.VMEM((ITERS, n_pieces, rows, WIDE), f32),
            pltpu.VMEM((n_slots * n_cell, rows, WIDE), f32),
            pltpu.VMEM((ITERS, n_slots * n_cell, rows, WIDE), f32),
            pltpu.VMEM((n, rows, 2 * LANES), f32),
            pltpu.VMEM((n, rows, cells), f32),
            pltpu.VMEM((ITERS, n, 2, rows, width), f32),
            pltpu.VMEM((ITERS, n, rows, width), f32),
            pltpu.VMEM((ITERS, n, n_chip, rows, width), f32),
            pltpu.VMEM((ITERS, n, 2, rows, width), f32),
            pltpu.VMEM((ITERS, n_cell, rows, 2 * LANES), f32),
            pltpu.VMEM((2 * LANES, 2 * LANES), f32),
            dma((ITERS, 2, n_pieces)),
            dma((ITERS, 2, n_pieces)),
            dma((ITERS, n_slots, n_cell - 1)),
            dma((ITERS, n_slots, n_cell - 1)),
            dma((ITERS, n)),
            dma((ITERS, n)),
            dma((ITERS, n, max(n_chip - 1, 1))),
            dma((ITERS, n, max(n_chip - 1, 1))),
            dma((ITERS, n)),
            dma((ITERS, n)),
            dma((ITERS, n_cell - 1)),
            dma((ITERS, n_cell - 1)),
            dma((cells // WIDE,)),
            dma((2,)),
            dma((n,)),
            dma((n,)),
        ],
        compiler_params=pltpu.CompilerParams(
            collective_id=0, has_side_effects=True, vmem_limit_bytes=60 * 1024 * 1024
        ),
    )(
        counts,
        usage_init.T.reshape(n, rows, cells),
        program.reshape(n, rows, genes),
    )
    usage = usage.reshape(k, cells).T
    program = program.reshape(k, genes)[:, :real_genes]
    return usage, program


def solution(mesh):
    return jax.shard_map(
        functools.partial(body, mesh),
        mesh=mesh,
        in_specs=(P("cell", "gene"), P(("rep", "cell"), None), P("rep", "gene")),
        out_specs=(P(("rep", "cell"), None), P("rep", "gene")),
        check_vma=False,
    )
```

```python
import functools

import jax
import jax.numpy as jnp
from jax import lax
from jax.experimental import pallas as pl
from jax.experimental.pallas import tpu as pltpu
from jax.sharding import PartitionSpec as P

ITERS = 2
LANES = 128
WIDE = 2 * LANES
HOP, PACE = 4, 1
GRAM_LAG, CORE_LAG, CHIP_LAG, SHARE_LAG = 5, 2, 7, 9
JOIN_LAG, SETTLE_LAG = 5, 4

MESH = pl.DeviceIdType.MESH
f32 = jnp.float32


def dot(left, right, left_dim, right_dim):
    return lax.dot_general(
        left,
        right,
        (((left_dim,), (right_dim,)), ((), ())),
        preferred_element_type=f32,
    )


def parts(x):
    high = x.astype(jnp.bfloat16)
    return high, (x - high.astype(f32)).astype(jnp.bfloat16)


def dot_exact_right(left, right, right_dim):
    rows = left.shape[0]
    both = dot(jnp.concatenate(parts(left), 0), right, 1, right_dim)
    return both[:rows] + both[rows:]


def dot_three(left, right, right_dim):
    rows = left.shape[0]
    left_high, left_low = parts(left)
    right_high, right_low = parts(right)
    both = dot(jnp.concatenate([left_high, left_low], 0), right_high, 1, right_dim)
    return both[:rows] + (both[rows:] + dot(left_high, right_low, 1, right_dim))


def gram_blocks(n, rows):
    return [(r, 0) for r in range(n)] + [(r, 1) for r in range(n) if (r + 1) * rows > LANES]


def kernel(
    sizes,
    counts_ref, u_ref, p_ref, u_out, p_out,
    counts, e_ref,
    u_buf, p_buf, zp, z_in, z_out, z_mid, z_fin, g_own, g_all, gram, below,
    c_send, c_in, x_buf, x_fin, last_gram, u_gram,
    zs_sem, zr_sem, gs_sem, gr_sem, cs_sem, cr_sem, xs_sem, xr_sem, fs_sem, fr_sem, ds_sem, dr_sem,
    in_sem, start_sem, u_sem, p_sem,
):
    n_gene, n_cell, n, rows, cells, genes, real_genes, n_slots = sizes
    k = n * rows
    n_chip, reach = n_cell // 2, n_gene // 2
    subs = cells // WIDE
    half_genes = genes // 2
    blocks = gram_blocks(n, rows)
    lead_chunk = -(-(n - 1) // subs)
    lead = lead_chunk * subs
    n_pieces = n * subs + n_slots
    final = n - 1

    z = lax.axis_index("gene")
    cell = lax.axis_index("cell")
    core = lax.rem(cell, 2)
    chip = cell // 2
    other = 1 - core
    low = z < reach
    far = jnp.where(low, reach - 1 - z, z - reach)
    inner = jnp.where(low, z + 1, z - 1)
    outer = jnp.where(low, z - 1, z + 1)
    middle, edge = far == 0, far == reach - 1

    def load(s):
        at_row = pl.ds(pl.multiple_of(s * WIDE, WIDE), WIDE)
        return pltpu.make_async_copy(counts_ref.at[at_row], counts.at[s], in_sem.at[s])

    load_program = pltpu.make_async_copy(p_ref, p_buf.at[0], start_sem.at[0])
    load_usage = pltpu.make_async_copy(u_ref, u_buf.at[0], start_sem.at[1])
    load_program.start()
    for s in range(subs):
        load(s).start()
    load_usage.start()

    barrier = pltpu.get_barrier_semaphore()
    pl.semaphore_signal(barrier, inc=1, device_id={"gene": inner}, device_id_type=MESH)

    @pl.when(jnp.logical_not(edge))
    def _():
        pl.semaphore_signal(barrier, inc=1, device_id={"gene": outer}, device_id_type=MESH)

    for away in range(1, n_cell):
        peer = lax.rem(cell + away, n_cell)
        pl.semaphore_signal(barrier, inc=1, device_id={"cell": peer}, device_id_type=MESH)

    def take_counts(s):
        load(s).wait()
        at_row = pl.ds(pl.multiple_of(s * WIDE, WIDE), WIDE)
        e_ref[at_row, :real_genes] = counts[s].astype(f32).astype(jnp.bfloat16)
        if real_genes < genes:
            e_ref[at_row, real_genes:] = jnp.zeros((WIDE, genes - real_genes), jnp.bfloat16)

    def clear(i, carry):
        u_buf[1 + i // n, lax.rem(i, n)] = jnp.zeros((rows, cells), f32)
        return carry

    lax.fori_loop(0, ITERS * n, clear, 0)
    load_program.wait()
    early = min(2, subs)
    lax.fori_loop(0, early, lambda s, carry: (take_counts(s), carry)[1], 0)
    pl.semaphore_wait(barrier, n_cell + 1 - jnp.where(edge, 1, 0))

    def remote(src, dst, send, recv, to):
        return pltpu.make_async_remote_copy(
            src_ref=src, dst_ref=dst, send_sem=send, recv_sem=recv, device_id=to, device_id_type=MESH
        )

    def inward(it, c):
        return remote(z_out.at[it, c], z_in.at[it, c], zs_sem.at[it, 0, c], zr_sem.at[it, 0, c], {"gene": inner})

    def across(it, c):
        return remote(z_out.at[it, c], z_mid.at[it, c], zs_sem.at[it, 0, c], zr_sem.at[it, 1, c], {"gene": inner})

    def outward(it, c):
        return remote(z_fin.at[it, c], z_fin.at[it, c], zs_sem.at[it, 1, c], zr_sem.at[it, 1, c], {"gene": outer})

    def spread(it, s, away):
        to = lax.rem(cell + away, n_cell)
        mine = g_all.at[it, s * n_cell + cell]
        return remote(mine, mine, gs_sem.at[it, s, away - 1], gr_sem.at[it, s, away - 1], {"cell": to})

    def spread_from(it, s, away):
        to = lax.rem(cell + n_cell - away, n_cell)
        theirs = g_all.at[it, s * n_cell + to]
        return remote(theirs, theirs, gs_sem.at[it, s, away - 1], gr_sem.at[it, s, away - 1], {"cell": to})

    def direct(it, away):
        to = lax.rem(cell + away, n_cell)
        mine = last_gram.at[it, cell]
        return remote(mine, mine, ds_sem.at[it, away - 1], dr_sem.at[it, away - 1], {"cell": to})

    def direct_from(it, away):
        to = lax.rem(cell + n_cell - away, n_cell)
        theirs = last_gram.at[it, to]
        return remote(theirs, theirs, ds_sem.at[it, away - 1], dr_sem.at[it, away - 1], {"cell": to})

    def columns(last):
        return pl.ds(0, half_genes if last else half_genes + LANES)

    def to_core(it, j, last):
        at = columns(last)
        return remote(
            c_send.at[it, j, other, :, at], c_in.at[it, j, :, at], cs_sem.at[it, j], cr_sem.at[it, j],
            {"cell": chip * 2 + other},
        )

    def to_chip(it, j, away, last):
        to = lax.rem(chip + away, n_chip)
        mine = x_buf.at[it, j, chip, :, columns(last)]
        return remote(mine, mine, xs_sem.at[it, j, away - 1], xr_sem.at[it, j, away - 1], {"cell": to * 2 + core})

    def from_chip(it, j, away, last):
        to = lax.rem(chip + n_chip - away, n_chip)
        theirs = x_buf.at[it, j, to, :, columns(last)]
        return remote(theirs, theirs, xs_sem.at[it, j, away - 1], xr_sem.at[it, j, away - 1], {"cell": to * 2 + core})

    def share(it, j, which, last):
        piece = x_fin.at[it, j, which, :, columns(last)]
        return remote(piece, piece, fs_sem.at[it, j], fr_sem.at[it, j], {"cell": chip * 2 + other})

    def put_usage(j):
        return pltpu.make_async_copy(u_buf.at[ITERS, j], u_out.at[j], u_sem.at[j])

    def put_program(j):
        return pltpu.make_async_copy(p_buf.at[ITERS, j], p_out.at[j], p_sem.at[j])

    def gather_in(it, c):
        @pl.when(edge)
        def _():
            z_out[it, c] = zp[c]

        @pl.when(jnp.logical_not(edge))
        def _():
            inward(it, c).wait_recv()
            z_out[it, c] = zp[c] + z_in[it, c]

        @pl.when(middle)
        def _():
            across(it, c).start()

        @pl.when(jnp.logical_not(middle))
        def _():
            inward(it, c).start()

    def spread_out(it, c):
        @pl.when(middle)
        def _():
            across(it, c).wait_recv()
            z_fin[it, c] = z_out[it, c] + z_mid[it, c]

        @pl.when(jnp.logical_not(middle))
        def _():
            outward(it, c).wait_recv()

        @pl.when(jnp.logical_not(edge))
        def _():
            outward(it, c).start()

    def numerator(it, q):
        j, s = q // subs, lax.rem(q, subs)
        at_row = pl.ds(pl.multiple_of(s * WIDE, WIDE), WIDE)
        zp[q + jnp.where(q >= lead, n_slots, 0)] = dot_exact_right(p_buf[it, j], e_ref[at_row, :], 1)

    def own_gram(it):
        whole = p_buf[it].reshape(k, genes)
        own = dot_three(whole, whole, 1)
        own = jnp.concatenate([own, jnp.zeros((k, 2 * LANES - k), f32)], 1)
        for i in range(2 * n_slots * n_cell):
            r, h = blocks[min(i, len(blocks) - 1)]
            at = (i % 2) * LANES
            g_own[i // 2, :, at:at + LANES] = own[r * rows:(r + 1) * rows, h * LANES:(h + 1) * LANES]
        for s in range(n_slots):
            zp[lead + s] = g_own[s * n_cell + cell]

    def spread_gram(it):
        for s in range(n_slots):
            g_all[it, s * n_cell + cell] = z_fin[it, lead + s]
            for away in range(1, n_cell):
                spread(it, s, away).start()

    def join_gram(it):
        for s in range(n_slots):
            for away in range(1, n_cell):
                spread_from(it, s, away).wait_recv()
        none = jnp.zeros((rows, LANES), f32)
        lines = []
        for r in range(n):
            halves = []
            for h in range(2):
                if (r, h) in blocks:
                    i = blocks.index((r, h))
                    halves.append(g_all[it, i // 2, :, (i % 2) * LANES:(i % 2 + 1) * LANES])
                else:
                    halves.append(none)
            lines.append(jnp.concatenate(halves, 1))
        lines.append(jnp.zeros((2 * LANES - k, 2 * LANES), f32))
        known = jnp.concatenate(lines, 0)
        first = min(r for r, h in blocks if h == 1) * rows
        row = lax.broadcasted_iota(jnp.int32, known.shape, 0)
        column = lax.broadcasted_iota(jnp.int32, known.shape, 1)
        missing = jnp.logical_and(row < first, column >= LANES)
        full = jnp.where(missing, known.T, known)
        for r in range(n):
            gram[r] = full[r * rows:(r + 1) * rows]

    def usage_below(it, j):
        below[j] = dot_three(gram[j][:, :k], u_buf[it].reshape(k, cells), 0)

    def update_usage(it, j, last):
        first = j * subs + jnp.where(j >= lead_chunk, n_slots, 0)
        top = jnp.concatenate([z_fin[it, first + s] for s in range(subs)], 1)
        new = u_buf[it, j] * top / below[j]
        u_buf[it + 1, j] = new

        @pl.when(it == ITERS - 1)
        def _():
            put_usage(j).start()

        def half(h):
            at = pl.ds(pl.multiple_of(h * half_genes, LANES), half_genes)
            c_send[it, j, h, :, :half_genes] = dot_exact_right(new, e_ref[:, at], 0)

        own = dot_three(new, u_buf[it + 1].reshape(k, cells), 1)
        pad = jnp.zeros((rows, 2 * LANES - k), f32)
        if last:
            last_gram[it, cell] = jnp.concatenate([own, pad], 1)
            for away in range(1, n_cell):
                direct(it, away).start()
        else:
            c_send[it, j, 0, :, half_genes:] = own[:, :LANES]
            c_send[it, j, 1, :, half_genes:] = jnp.concatenate([own[:, LANES:], pad], 1)
        half(other)
        to_core(it, j, last).start()
        half(core)

    def join_core(it, j, last):
        at = columns(last)
        to_core(it, j, last).wait_recv()
        x_buf[it, j, chip, :, at] = c_send[it, j, core, :, at] + c_in[it, j, :, at]
        for away in range(1, n_chip):
            to_chip(it, j, away, last).start()

    def join_chip(it, j, last):
        at = columns(last)
        for away in range(1, n_chip):
            from_chip(it, j, away, last).wait_recv()
        total = x_buf[it, j, 0, :, at]
        for peer in range(1, n_chip):
            total = total + x_buf[it, j, peer, :, at]
        x_fin[it, j, core, :, at] = total
        share(it, j, core, last).start()

    def join_share(it, j, last):
        share(it, j, other, last).wait_recv()

    def join_usage_gram(it):
        for away in range(1, n_cell):
            direct_from(it, away).wait_recv()
        ending = last_gram[it, 0]
        for peer in range(1, n_cell):
            ending = ending + last_gram[it, peer]
        at_column = lax.broadcasted_iota(jnp.int32, (rows, 2 * LANES), 1)
        lower, strict = [], []
        for r in range(n):
            if r == final:
                block = ending
            else:
                block = jnp.concatenate([x_fin[it, r, h, :, half_genes:] for h in range(2)], 1)
            lower.append(jnp.where(at_column < (r + 1) * rows, block, 0.0))
            strict.append(jnp.where(at_column < r * rows, block, 0.0))
        pad = jnp.zeros((2 * LANES - k, 2 * LANES), f32)
        u_gram[...] = jnp.concatenate(lower + [pad], 0) + jnp.concatenate(strict + [pad], 0).T

    def update_program(it, j):
        top = jnp.concatenate([x_fin[it, j, h, :, :half_genes] for h in range(2)], 1)
        old = p_buf[it].reshape(k, genes)
        at_row = pl.ds(pl.multiple_of(j * rows, rows), rows)
        new = p_buf[it, j] * top / dot_three(u_gram[at_row, :][:, :k], old, 0)
        if real_genes < genes:
            inside = lax.broadcasted_iota(jnp.int32, (rows, genes), 1) < real_genes
            new = jnp.where(inside, new, 0.0)
        p_buf[it + 1, j] = new

        @pl.when(it == ITERS - 1)
        def _():
            put_program(j).start()

    def settle_pieces(it):
        def pieces(c, carry):
            inward(it, c).wait_send()

            @pl.when(jnp.logical_not(edge))
            def _():
                outward(it, c).wait_send()

            return carry

        lax.fori_loop(0, n_pieces, pieces, 0)
        for s in range(n_slots):
            for away in range(1, n_cell):
                spread(it, s, away).wait_send()

    def settle_chunks(it):
        def chunks(j, last):
            to_core(it, j, last).wait_send()
            for away in range(1, n_chip):
                to_chip(it, j, away, last).wait_send()
            share(it, j, core, last).wait_send()

        lax.fori_loop(0, final, lambda j, carry: (chunks(j, False), carry)[1], 0)
        chunks(final, True)
        for away in range(1, n_cell):
            direct(it, away).wait_send()

    place = [(j + 1) * subs - 1 + (n_slots if j >= lead_chunk else 0) for j in range(n)]
    gram_place = PACE * (lead + n_slots - 1)
    joined = gram_place + GRAM_LAG
    turns = [max(PACE * place[j], joined + 1 + 2 * j) for j in range(n)]
    below_turns = [joined + 2 * j for j in range(n)]
    inward_lag = (reach - 1 - far) * HOP
    done = (reach + far) * HOP
    period = (2 * reach - 1) * HOP + turns[final] + JOIN_LAG
    ticks = ITERS * period + n
    pace_in = jnp.where(edge, 1, PACE)

    def tick(t, carry):
        def frame(start):
            it = 0
            for i in range(1, ITERS):
                it = it + jnp.where(t >= start + i * period, 1, 0)
            return it, t - start - it * period

        def at_turn(start, when, act):
            it, since = frame(start)
            hit, j = since == when[0], 0
            for i in range(1, len(when)):
                now = since == when[i]
                hit, j = jnp.logical_or(hit, now), jnp.where(now, i, j)

            @pl.when(hit)
            def _():
                act(it, j)

        def at_chunk(start, when, lag, last_lag, act):
            at_turn(start + lag, when[:final], lambda it, j: act(it, j, False))
            at_turn(start + last_lag, when[final:], lambda it, j: act(it, final, True))

        def at_time(start, act):
            at_turn(start, [0], lambda it, j: act(it))

        @pl.when(jnp.logical_and(t >= early, t < subs))
        def _():
            take_counts(t)

        at_chunk(done, turns, CORE_LAG, CORE_LAG, join_core)
        at_chunk(done, turns, CHIP_LAG, JOIN_LAG + 2, join_chip)
        at_chunk(done, turns, SHARE_LAG, JOIN_LAG + final, join_share)
        at_time(period, join_usage_gram)
        at_turn(period, list(range(n)), update_program)

        it, since = frame(0)
        q = since - jnp.where(since >= lead + n_slots, n_slots, 0)

        @pl.when(jnp.logical_and(jnp.logical_or(since < lead, since >= lead + n_slots), q < n * subs))
        def _():
            numerator(it, q)

        @pl.when(since == lead)
        def _():
            own_gram(it)

        def at_pieces(start, pace, act):
            it, since = frame(start)
            c = since // pace

            @pl.when(jnp.logical_and(jnp.logical_and(since >= 0, c * pace == since), c < n_pieces))
            def _():
                act(it, c)

        it_in, since_in = frame(inward_lag)
        c_in_turn = jnp.where(edge, since_in, since_in // PACE)

        @pl.when(
            jnp.logical_and(
                jnp.logical_and(since_in >= 0, c_in_turn * pace_in == since_in), c_in_turn < n_pieces
            )
        )
        def _():
            gather_in(it_in, c_in_turn)

        at_pieces(done, PACE, spread_out)
        at_time(done + gram_place, spread_gram)
        at_time(done + joined, join_gram)
        at_turn(done, below_turns, usage_below)
        at_chunk(done, turns, 0, 0, update_usage)
        at_time(done + turns[final] + SETTLE_LAG, settle_pieces)
        return carry

    load_usage.wait()
    lax.fori_loop(0, ticks, tick, 0)

    for it in range(ITERS):
        settle_chunks(it)
    for j in range(n):
        put_usage(j).wait()
        put_program(j).wait()


def body(mesh, counts, usage_init, program_init):
    cells, k = usage_init.shape
    real_genes = program_init.shape[1]
    n_gene, n_cell = mesh.shape["gene"], mesh.shape["cell"]
    n_chip = n_cell // 2
    rows = max(r for r in range(8, 41, 8) if k % r == 0)
    n = k // rows
    genes = -(-real_genes // (2 * LANES)) * 2 * LANES
    n_slots = -(-len(gram_blocks(n, rows)) // (2 * n_cell))
    n_pieces = n * (cells // WIDE) + n_slots
    width = genes // 2 + LANES

    program = program_init
    if genes > real_genes:
        program = jnp.pad(program, ((0, 0), (0, genes - real_genes)))

    sizes = (n_gene, n_cell, n, rows, cells, genes, real_genes, n_slots)
    anywhere = pl.BlockSpec(memory_space=pl.ANY)
    dma = pltpu.SemaphoreType.DMA
    usage, program = pl.pallas_call(
        functools.partial(kernel, sizes),
        out_shape=[
            jax.ShapeDtypeStruct((n, rows, cells), f32),
            jax.ShapeDtypeStruct((n, rows, genes), f32),
        ],
        in_specs=[anywhere] * 3,
        out_specs=[anywhere] * 2,
        scratch_shapes=[
            pltpu.VMEM((cells // WIDE, WIDE, real_genes), jnp.int32),
            pltpu.VMEM((cells, genes), jnp.bfloat16),
            pltpu.VMEM((ITERS + 1, n, rows, cells), f32),
            pltpu.VMEM((ITERS + 1, n, rows, genes), f32),
            pltpu.VMEM((n_pieces, rows, WIDE), f32),
            pltpu.VMEM((ITERS, n_pieces, rows, WIDE), f32),
            pltpu.VMEM((ITERS, n_pieces, rows, WIDE), f32),
            pltpu.VMEM((ITERS, n_pieces, rows, WIDE), f32),
            pltpu.VMEM((ITERS, n_pieces, rows, WIDE), f32),
            pltpu.VMEM((n_slots * n_cell, rows, WIDE), f32),
            pltpu.VMEM((ITERS, n_slots * n_cell, rows, WIDE), f32),
            pltpu.VMEM((n, rows, 2 * LANES), f32),
            pltpu.VMEM((n, rows, cells), f32),
            pltpu.VMEM((ITERS, n, 2, rows, width), f32),
            pltpu.VMEM((ITERS, n, rows, width), f32),
            pltpu.VMEM((ITERS, n, n_chip, rows, width), f32),
            pltpu.VMEM((ITERS, n, 2, rows, width), f32),
            pltpu.VMEM((ITERS, n_cell, rows, 2 * LANES), f32),
            pltpu.VMEM((2 * LANES, 2 * LANES), f32),
            dma((ITERS, 2, n_pieces)),
            dma((ITERS, 2, n_pieces)),
            dma((ITERS, n_slots, n_cell - 1)),
            dma((ITERS, n_slots, n_cell - 1)),
            dma((ITERS, n)),
            dma((ITERS, n)),
            dma((ITERS, n, max(n_chip - 1, 1))),
            dma((ITERS, n, max(n_chip - 1, 1))),
            dma((ITERS, n)),
            dma((ITERS, n)),
            dma((ITERS, n_cell - 1)),
            dma((ITERS, n_cell - 1)),
            dma((cells // WIDE,)),
            dma((2,)),
            dma((n,)),
            dma((n,)),
        ],
        compiler_params=pltpu.CompilerParams(
            collective_id=0, has_side_effects=True, vmem_limit_bytes=60 * 1024 * 1024
        ),
    )(
        counts,
        usage_init.T.reshape(n, rows, cells),
        program.reshape(n, rows, genes),
    )
    usage = usage.reshape(k, cells).T
    program = program.reshape(k, genes)[:, :real_genes]
    return usage, program


def solution(mesh):
    return jax.shard_map(
        functools.partial(body, mesh),
        mesh=mesh,
        in_specs=(P("cell", "gene"), P(("rep", "cell"), None), P("rep", "gene")),
        out_specs=(P(("rep", "cell"), None), P("rep", "gene")),
        check_vma=False,
    )
```

```python
import functools

import jax
import jax.numpy as jnp
from jax import lax
from jax.experimental import pallas as pl
from jax.experimental.pallas import tpu as pltpu
from jax.sharding import PartitionSpec as P

ITERS = 2
LANES = 128
WIDE = 2 * LANES
HOP, PACE = 4, 1
GRAM_LAG, CORE_LAG, CHIP_LAG, SHARE_LAG = 4, 2, 7, 9
JOIN_LAG, SETTLE_LAG = 5, 4

MESH = pl.DeviceIdType.MESH
f32 = jnp.float32


def dot(left, right, left_dim, right_dim):
    return lax.dot_general(
        left,
        right,
        (((left_dim,), (right_dim,)), ((), ())),
        preferred_element_type=f32,
    )


def parts(x):
    high = x.astype(jnp.bfloat16)
    return high, (x - high.astype(f32)).astype(jnp.bfloat16)


def dot_exact_right(left, right, right_dim):
    rows = left.shape[0]
    both = dot(jnp.concatenate(parts(left), 0), right, 1, right_dim)
    return both[:rows] + both[rows:]


def dot_three(left, right, right_dim):
    rows = left.shape[0]
    left_high, left_low = parts(left)
    right_high, right_low = parts(right)
    both = dot(jnp.concatenate([left_high, left_low], 0), right_high, 1, right_dim)
    return both[:rows] + (both[rows:] + dot(left_high, right_low, 1, right_dim))


def gram_blocks(n, rows):
    return [(r, 0) for r in range(n)] + [(r, 1) for r in range(n) if (r + 1) * rows > LANES]


def kernel(
    sizes,
    counts_ref, u_ref, p_ref, u_out, p_out,
    counts, e_ref,
    u_buf, p_buf, zp, z_in, z_out, z_mid, z_fin, g_own, g_all, gram, below,
    c_send, c_in, x_buf, x_fin, last_gram, u_gram,
    zs_sem, zr_sem, gs_sem, gr_sem, cs_sem, cr_sem, xs_sem, xr_sem, fs_sem, fr_sem, ds_sem, dr_sem,
    in_sem, start_sem, u_sem, p_sem,
):
    n_gene, n_cell, n, rows, cells, genes, real_genes, n_slots = sizes
    k = n * rows
    n_chip, reach = n_cell // 2, n_gene // 2
    subs = cells // WIDE
    half_genes = genes // 2
    blocks = gram_blocks(n, rows)
    lead_chunk = -(-(n - 1) // subs)
    lead = lead_chunk * subs
    n_pieces = n * subs + n_slots
    final = n - 1

    z = lax.axis_index("gene")
    cell = lax.axis_index("cell")
    core = lax.rem(cell, 2)
    chip = cell // 2
    other = 1 - core
    low = z < reach
    far = jnp.where(low, reach - 1 - z, z - reach)
    inner = jnp.where(low, z + 1, z - 1)
    outer = jnp.where(low, z - 1, z + 1)
    middle, edge = far == 0, far == reach - 1

    def load(s):
        at_row = pl.ds(pl.multiple_of(s * WIDE, WIDE), WIDE)
        return pltpu.make_async_copy(counts_ref.at[at_row], counts.at[s], in_sem.at[s])

    load_program = pltpu.make_async_copy(p_ref, p_buf.at[0], start_sem.at[0])
    load_usage = pltpu.make_async_copy(u_ref, u_buf.at[0], start_sem.at[1])
    load_program.start()
    for s in range(subs):
        load(s).start()
    load_usage.start()

    barrier = pltpu.get_barrier_semaphore()
    pl.semaphore_signal(barrier, inc=1, device_id={"gene": inner}, device_id_type=MESH)

    @pl.when(jnp.logical_not(edge))
    def _():
        pl.semaphore_signal(barrier, inc=1, device_id={"gene": outer}, device_id_type=MESH)

    for away in range(1, n_cell):
        peer = lax.rem(cell + away, n_cell)
        pl.semaphore_signal(barrier, inc=1, device_id={"cell": peer}, device_id_type=MESH)

    def take_counts(s):
        load(s).wait()
        at_row = pl.ds(pl.multiple_of(s * WIDE, WIDE), WIDE)
        e_ref[at_row, :real_genes] = counts[s].astype(f32).astype(jnp.bfloat16)
        if real_genes < genes:
            e_ref[at_row, real_genes:] = jnp.zeros((WIDE, genes - real_genes), jnp.bfloat16)

    def clear(i, carry):
        u_buf[1 + i // n, lax.rem(i, n)] = jnp.zeros((rows, cells), f32)
        return carry

    lax.fori_loop(0, ITERS * n, clear, 0)
    load_program.wait()
    early = min(2, subs)
    lax.fori_loop(0, early, lambda s, carry: (take_counts(s), carry)[1], 0)
    pl.semaphore_wait(barrier, n_cell + 1 - jnp.where(edge, 1, 0))

    def remote(src, dst, send, recv, to):
        return pltpu.make_async_remote_copy(
            src_ref=src, dst_ref=dst, send_sem=send, recv_sem=recv, device_id=to, device_id_type=MESH
        )

    def inward(it, c):
        return remote(z_out.at[it, c], z_in.at[it, c], zs_sem.at[it, 0, c], zr_sem.at[it, 0, c], {"gene": inner})

    def across(it, c):
        return remote(z_out.at[it, c], z_mid.at[it, c], zs_sem.at[it, 0, c], zr_sem.at[it, 1, c], {"gene": inner})

    def outward(it, c):
        return remote(z_fin.at[it, c], z_fin.at[it, c], zs_sem.at[it, 1, c], zr_sem.at[it, 1, c], {"gene": outer})

    def spread(it, s, away):
        to = lax.rem(cell + away, n_cell)
        mine = g_all.at[it, s * n_cell + cell]
        return remote(mine, mine, gs_sem.at[it, s, away - 1], gr_sem.at[it, s, away - 1], {"cell": to})

    def spread_from(it, s, away):
        to = lax.rem(cell + n_cell - away, n_cell)
        theirs = g_all.at[it, s * n_cell + to]
        return remote(theirs, theirs, gs_sem.at[it, s, away - 1], gr_sem.at[it, s, away - 1], {"cell": to})

    def direct(it, away):
        to = lax.rem(cell + away, n_cell)
        mine = last_gram.at[it, cell]
        return remote(mine, mine, ds_sem.at[it, away - 1], dr_sem.at[it, away - 1], {"cell": to})

    def direct_from(it, away):
        to = lax.rem(cell + n_cell - away, n_cell)
        theirs = last_gram.at[it, to]
        return remote(theirs, theirs, ds_sem.at[it, away - 1], dr_sem.at[it, away - 1], {"cell": to})

    def columns(last):
        return pl.ds(0, half_genes if last else half_genes + LANES)

    def to_core(it, j, last):
        at = columns(last)
        return remote(
            c_send.at[it, j, other, :, at], c_in.at[it, j, :, at], cs_sem.at[it, j], cr_sem.at[it, j],
            {"cell": chip * 2 + other},
        )

    def to_chip(it, j, away, last):
        to = lax.rem(chip + away, n_chip)
        mine = x_buf.at[it, j, chip, :, columns(last)]
        return remote(mine, mine, xs_sem.at[it, j, away - 1], xr_sem.at[it, j, away - 1], {"cell": to * 2 + core})

    def from_chip(it, j, away, last):
        to = lax.rem(chip + n_chip - away, n_chip)
        theirs = x_buf.at[it, j, to, :, columns(last)]
        return remote(theirs, theirs, xs_sem.at[it, j, away - 1], xr_sem.at[it, j, away - 1], {"cell": to * 2 + core})

    def share(it, j, which, last):
        piece = x_fin.at[it, j, which, :, columns(last)]
        return remote(piece, piece, fs_sem.at[it, j], fr_sem.at[it, j], {"cell": chip * 2 + other})

    def put_usage(j):
        return pltpu.make_async_copy(u_buf.at[ITERS, j], u_out.at[j], u_sem.at[j])

    def put_program(j):
        return pltpu.make_async_copy(p_buf.at[ITERS, j], p_out.at[j], p_sem.at[j])

    def gather_in(it, c):
        @pl.when(edge)
        def _():
            z_out[it, c] = zp[c]

        @pl.when(jnp.logical_not(edge))
        def _():
            inward(it, c).wait_recv()
            z_out[it, c] = zp[c] + z_in[it, c]

        @pl.when(middle)
        def _():
            across(it, c).start()

        @pl.when(jnp.logical_not(middle))
        def _():
            inward(it, c).start()

    def spread_out(it, c):
        @pl.when(middle)
        def _():
            across(it, c).wait_recv()
            z_fin[it, c] = z_out[it, c] + z_mid[it, c]

        @pl.when(jnp.logical_not(middle))
        def _():
            outward(it, c).wait_recv()

        @pl.when(jnp.logical_not(edge))
        def _():
            outward(it, c).start()

    def numerator(it, q):
        j, s = q // subs, lax.rem(q, subs)
        at_row = pl.ds(pl.multiple_of(s * WIDE, WIDE), WIDE)
        zp[q + jnp.where(q >= lead, n_slots, 0)] = dot_exact_right(p_buf[it, j], e_ref[at_row, :], 1)

    def own_gram(it):
        whole = p_buf[it].reshape(k, genes)
        own = dot_three(whole, whole, 1)
        own = jnp.concatenate([own, jnp.zeros((k, 2 * LANES - k), f32)], 1)
        for i in range(2 * n_slots * n_cell):
            r, h = blocks[min(i, len(blocks) - 1)]
            at = (i % 2) * LANES
            g_own[i // 2, :, at:at + LANES] = own[r * rows:(r + 1) * rows, h * LANES:(h + 1) * LANES]
        for s in range(n_slots):
            zp[lead + s] = g_own[s * n_cell + cell]

    def spread_gram(it):
        for s in range(n_slots):
            g_all[it, s * n_cell + cell] = z_fin[it, lead + s]
            for away in range(1, n_cell):
                spread(it, s, away).start()

    def join_gram(it):
        for s in range(n_slots):
            for away in range(1, n_cell):
                spread_from(it, s, away).wait_recv()
        none = jnp.zeros((rows, LANES), f32)
        lines = []
        for r in range(n):
            halves = []
            for h in range(2):
                if (r, h) in blocks:
                    i = blocks.index((r, h))
                    halves.append(g_all[it, i // 2, :, (i % 2) * LANES:(i % 2 + 1) * LANES])
                else:
                    halves.append(none)
            lines.append(jnp.concatenate(halves, 1))
        lines.append(jnp.zeros((2 * LANES - k, 2 * LANES), f32))
        known = jnp.concatenate(lines, 0)
        first = min(r for r, h in blocks if h == 1) * rows
        row = lax.broadcasted_iota(jnp.int32, known.shape, 0)
        column = lax.broadcasted_iota(jnp.int32, known.shape, 1)
        missing = jnp.logical_and(row < first, column >= LANES)
        full = jnp.where(missing, known.T, known)
        for r in range(n):
            gram[r] = full[r * rows:(r + 1) * rows]

    def usage_below(it, j):
        below[j] = dot_three(gram[j][:, :k], u_buf[it].reshape(k, cells), 0)

    def update_usage(it, j, last):
        first = j * subs + jnp.where(j >= lead_chunk, n_slots, 0)
        top = jnp.concatenate([z_fin[it, first + s] for s in range(subs)], 1)
        new = u_buf[it, j] * top / below[j]
        u_buf[it + 1, j] = new

        @pl.when(it == ITERS - 1)
        def _():
            put_usage(j).start()

        def half(h):
            at = pl.ds(pl.multiple_of(h * half_genes, LANES), half_genes)
            c_send[it, j, h, :, :half_genes] = dot_exact_right(new, e_ref[:, at], 0)

        own = dot_three(new, u_buf[it + 1].reshape(k, cells), 1)
        pad = jnp.zeros((rows, 2 * LANES - k), f32)
        if last:
            last_gram[it, cell] = jnp.concatenate([own, pad], 1)
            for away in range(1, n_cell):
                direct(it, away).start()
        else:
            c_send[it, j, 0, :, half_genes:] = own[:, :LANES]
            c_send[it, j, 1, :, half_genes:] = jnp.concatenate([own[:, LANES:], pad], 1)
        half(other)
        to_core(it, j, last).start()
        half(core)

    def join_core(it, j, last):
        at = columns(last)
        to_core(it, j, last).wait_recv()
        x_buf[it, j, chip, :, at] = c_send[it, j, core, :, at] + c_in[it, j, :, at]
        for away in range(1, n_chip):
            to_chip(it, j, away, last).start()

    def join_chip(it, j, last):
        at = columns(last)
        for away in range(1, n_chip):
            from_chip(it, j, away, last).wait_recv()
        total = x_buf[it, j, 0, :, at]
        for peer in range(1, n_chip):
            total = total + x_buf[it, j, peer, :, at]
        x_fin[it, j, core, :, at] = total
        share(it, j, core, last).start()

    def join_share(it, j, last):
        share(it, j, other, last).wait_recv()

    def join_usage_gram(it):
        for away in range(1, n_cell):
            direct_from(it, away).wait_recv()
        ending = last_gram[it, 0]
        for peer in range(1, n_cell):
            ending = ending + last_gram[it, peer]
        at_column = lax.broadcasted_iota(jnp.int32, (rows, 2 * LANES), 1)
        lower, strict = [], []
        for r in range(n):
            if r == final:
                block = ending
            else:
                block = jnp.concatenate([x_fin[it, r, h, :, half_genes:] for h in range(2)], 1)
            lower.append(jnp.where(at_column < (r + 1) * rows, block, 0.0))
            strict.append(jnp.where(at_column < r * rows, block, 0.0))
        pad = jnp.zeros((2 * LANES - k, 2 * LANES), f32)
        u_gram[...] = jnp.concatenate(lower + [pad], 0) + jnp.concatenate(strict + [pad], 0).T

    def update_program(it, j):
        top = jnp.concatenate([x_fin[it, j, h, :, :half_genes] for h in range(2)], 1)
        old = p_buf[it].reshape(k, genes)
        at_row = pl.ds(pl.multiple_of(j * rows, rows), rows)
        new = p_buf[it, j] * top / dot_three(u_gram[at_row, :][:, :k], old, 0)
        if real_genes < genes:
            inside = lax.broadcasted_iota(jnp.int32, (rows, genes), 1) < real_genes
            new = jnp.where(inside, new, 0.0)
        p_buf[it + 1, j] = new

        @pl.when(it == ITERS - 1)
        def _():
            put_program(j).start()

    def settle_pieces(it):
        def pieces(c, carry):
            inward(it, c).wait_send()

            @pl.when(jnp.logical_not(edge))
            def _():
                outward(it, c).wait_send()

            return carry

        lax.fori_loop(0, n_pieces, pieces, 0)
        for s in range(n_slots):
            for away in range(1, n_cell):
                spread(it, s, away).wait_send()

    def settle_chunks(it):
        def chunks(j, last):
            to_core(it, j, last).wait_send()
            for away in range(1, n_chip):
                to_chip(it, j, away, last).wait_send()
            share(it, j, core, last).wait_send()

        lax.fori_loop(0, final, lambda j, carry: (chunks(j, False), carry)[1], 0)
        chunks(final, True)
        for away in range(1, n_cell):
            direct(it, away).wait_send()

    place = [(j + 1) * subs - 1 + (n_slots if j >= lead_chunk else 0) for j in range(n)]
    gram_place = PACE * (lead + n_slots - 1)
    joined = gram_place + GRAM_LAG
    turns = [max(PACE * place[j], joined + 1 + 2 * j) for j in range(n)]
    below_turns = [joined + 2 * j for j in range(n)]
    inward_lag = (reach - 1 - far) * HOP
    done = (reach + far) * HOP
    period = (2 * reach - 1) * HOP + turns[final] + JOIN_LAG
    ticks = ITERS * period + n
    pace_in = jnp.where(edge, 1, PACE)

    def tick(t, carry):
        def frame(start):
            it = 0
            for i in range(1, ITERS):
                it = it + jnp.where(t >= start + i * period, 1, 0)
            return it, t - start - it * period

        def at_turn(start, when, act):
            it, since = frame(start)
            hit, j = since == when[0], 0
            for i in range(1, len(when)):
                now = since == when[i]
                hit, j = jnp.logical_or(hit, now), jnp.where(now, i, j)

            @pl.when(hit)
            def _():
                act(it, j)

        def at_chunk(start, when, lag, last_lag, act):
            at_turn(start + lag, when[:final], lambda it, j: act(it, j, False))
            at_turn(start + last_lag, when[final:], lambda it, j: act(it, final, True))

        def at_time(start, act):
            at_turn(start, [0], lambda it, j: act(it))

        @pl.when(jnp.logical_and(t >= early, t < subs))
        def _():
            take_counts(t)

        turn = frame(done)[1]
        opening = frame(period)[1]

        @pl.when(turn >= turns[0] + SHARE_LAG)
        def _():
            at_chunk(done, turns, SHARE_LAG, JOIN_LAG + final, join_share)

        @pl.when(jnp.logical_and(opening >= 0, opening < n))
        def _():
            at_time(period, join_usage_gram)
            at_turn(period, list(range(n)), update_program)

        it, since = frame(0)
        q = since - jnp.where(since >= lead + n_slots, n_slots, 0)

        @pl.when(jnp.logical_and(jnp.logical_or(since < lead, since >= lead + n_slots), q < n * subs))
        def _():
            numerator(it, q)

        @pl.when(since == lead)
        def _():
            own_gram(it)

        def at_pieces(start, pace, act):
            it, since = frame(start)
            c = since // pace

            @pl.when(jnp.logical_and(jnp.logical_and(since >= 0, c * pace == since), c < n_pieces))
            def _():
                act(it, c)

        it_in, since_in = frame(inward_lag)
        c_in_turn = jnp.where(edge, since_in, since_in // PACE)

        @pl.when(
            jnp.logical_and(
                jnp.logical_and(since_in >= 0, c_in_turn * pace_in == since_in), c_in_turn < n_pieces
            )
        )
        def _():
            gather_in(it_in, c_in_turn)

        at_pieces(done, PACE, spread_out)

        @pl.when(turn >= turns[0] + CORE_LAG)
        def _():
            at_chunk(done, turns, CORE_LAG, CORE_LAG, join_core)
            at_chunk(done, turns, CHIP_LAG, JOIN_LAG + 2, join_chip)

        @pl.when(turn >= gram_place)
        def _():
            at_time(done + gram_place, spread_gram)
            at_time(done + joined, join_gram)
            at_turn(done, below_turns, usage_below)
            at_chunk(done, turns, 0, 0, update_usage)
            at_time(done + turns[final] + SETTLE_LAG, settle_pieces)

        return carry

    load_usage.wait()
    lax.fori_loop(0, ticks, tick, 0)

    for it in range(ITERS):
        settle_chunks(it)
    for j in range(n):
        put_usage(j).wait()
        put_program(j).wait()


def hand_over(n, u_ref, p_ref, u_out, p_out, sem):
    moves = [
        pltpu.make_async_copy(src.at[j], dst.at[j], sem.at[i, j])
        for i, (src, dst) in enumerate([(p_ref, p_out), (u_ref, u_out)])
        for j in range(n)
    ]
    for move in moves:
        move.start()
    for move in moves:
        move.wait()


def body(mesh, counts, usage_init, program_init):
    cells, k = usage_init.shape
    real_genes = program_init.shape[1]
    n_gene, n_cell = mesh.shape["gene"], mesh.shape["cell"]
    n_chip = n_cell // 2
    rows = max(r for r in range(8, 41, 8) if k % r == 0)
    n = k // rows
    genes = -(-real_genes // (2 * LANES)) * 2 * LANES
    n_slots = -(-len(gram_blocks(n, rows)) // (2 * n_cell))
    n_pieces = n * (cells // WIDE) + n_slots
    width = genes // 2 + LANES

    program = program_init
    if genes > real_genes:
        program = jnp.pad(program, ((0, 0), (0, genes - real_genes)))

    sizes = (n_gene, n_cell, n, rows, cells, genes, real_genes, n_slots)
    anywhere = pl.BlockSpec(memory_space=pl.ANY)
    in_hbm = pl.BlockSpec(memory_space=pltpu.HBM)
    dma = pltpu.SemaphoreType.DMA
    usage, program = pl.pallas_call(
        functools.partial(kernel, sizes),
        out_shape=[
            jax.ShapeDtypeStruct((n, rows, cells), f32),
            jax.ShapeDtypeStruct((n, rows, genes), f32),
        ],
        in_specs=[in_hbm] * 3,
        out_specs=[anywhere] * 2,
        scratch_shapes=[
            pltpu.VMEM((cells // WIDE, WIDE, real_genes), jnp.int32),
            pltpu.VMEM((cells, genes), jnp.bfloat16),
            pltpu.VMEM((ITERS + 1, n, rows, cells), f32),
            pltpu.VMEM((ITERS + 1, n, rows, genes), f32),
            pltpu.VMEM((n_pieces, rows, WIDE), f32),
            pltpu.VMEM((ITERS, n_pieces, rows, WIDE), f32),
            pltpu.VMEM((ITERS, n_pieces, rows, WIDE), f32),
            pltpu.VMEM((ITERS, n_pieces, rows, WIDE), f32),
            pltpu.VMEM((ITERS, n_pieces, rows, WIDE), f32),
            pltpu.VMEM((n_slots * n_cell, rows, WIDE), f32),
            pltpu.VMEM((ITERS, n_slots * n_cell, rows, WIDE), f32),
            pltpu.VMEM((n, rows, 2 * LANES), f32),
            pltpu.VMEM((n, rows, cells), f32),
            pltpu.VMEM((ITERS, n, 2, rows, width), f32),
            pltpu.VMEM((ITERS, n, rows, width), f32),
            pltpu.VMEM((ITERS, n, n_chip, rows, width), f32),
            pltpu.VMEM((ITERS, n, 2, rows, width), f32),
            pltpu.VMEM((ITERS, n_cell, rows, 2 * LANES), f32),
            pltpu.VMEM((2 * LANES, 2 * LANES), f32),
            dma((ITERS, 2, n_pieces)),
            dma((ITERS, 2, n_pieces)),
            dma((ITERS, n_slots, n_cell - 1)),
            dma((ITERS, n_slots, n_cell - 1)),
            dma((ITERS, n)),
            dma((ITERS, n)),
            dma((ITERS, n, max(n_chip - 1, 1))),
            dma((ITERS, n, max(n_chip - 1, 1))),
            dma((ITERS, n)),
            dma((ITERS, n)),
            dma((ITERS, n_cell - 1)),
            dma((ITERS, n_cell - 1)),
            dma((cells // WIDE,)),
            dma((2,)),
            dma((n,)),
            dma((n,)),
        ],
        compiler_params=pltpu.CompilerParams(
            collective_id=0, has_side_effects=True, vmem_limit_bytes=48 * 1024 * 1024
        ),
    )(
        counts,
        usage_init.T.reshape(n, rows, cells),
        program.reshape(n, rows, genes),
    )
    usage, program = pl.pallas_call(
        functools.partial(hand_over, n),
        out_shape=[
            jax.ShapeDtypeStruct((n, rows, cells), f32),
            jax.ShapeDtypeStruct((n, rows, genes), f32),
        ],
        in_specs=[anywhere] * 2,
        out_specs=[in_hbm] * 2,
        scratch_shapes=[dma((2, n))],
        compiler_params=pltpu.CompilerParams(vmem_limit_bytes=1024 * 1024),
    )(usage, program)
    usage = usage.reshape(k, cells).T
    program = program.reshape(k, genes)[:, :real_genes]
    return usage, program


def solution(mesh):
    return jax.shard_map(
        functools.partial(body, mesh),
        mesh=mesh,
        in_specs=(P("cell", "gene"), P(("rep", "cell"), None), P("rep", "gene")),
        out_specs=(P(("rep", "cell"), None), P("rep", "gene")),
        check_vma=False,
    )
```
